32 devices in a mesh: seq: 8 (over z, y), head: 4 (over x, core).
Axes of the slice: x: 2, y: 2, z: 4, core: 2. Of those that a mesh axis runs over, the one named last changes fastest.
Arguments:
- queries: bfloat16 [8192, 1024], P('seq', 'head'), may hold values from -6 to 6
- keys_values: bfloat16 [8192, 128], P('seq'), may hold values from -6 to 6
- init_state: float32 [64, 2080], replicated, may hold values from -48 to 48
- out_grad: bfloat16 [8192, 1024], P('seq', 'head'), may hold values from -6 to 6
Outputs:
- attended: bfloat16 [8192, 1024], P('seq', 'head')
- query_grad: bfloat16 [8192, 1024], P('seq', 'head')
- kv_grad: float32 [8192, 128], P('seq')
- init_grad: float32 [64, 2080], P(None, 'head')
The draws below stay inside these ranges and needn't reach their ends.
All inputs are finite; a program needn't handle non-finite values.
Results may differ from the reference program's by a relative error of at most 0.0071.
Values sent between devices are 32-bit elements; how exact they have to be, the bound alone decides.
A program may use at most 128 MiB of HBM per device.

```python
import jax
import jax.numpy as jnp
import numpy as np
from jax import lax

HEADS = 16
HEAD_DIM = 64
FEATURES = 2080
GROUP = 1024
TOKENS = 8192


def steps_of(rng, dims, shards, least, high):
    level, own = 1.0, jax.random.fold_in(rng, 6)
    for axis_at, blocks in shards:
        steps = jnp.exp(jax.random.uniform(jax.random.fold_in(own, axis_at), (blocks,), jnp.float32, least / len(shards), high / len(shards)))
        level = level * jnp.repeat(steps, dims[axis_at] // blocks).reshape([-1 if axis == axis_at else 1 for axis in range(len(dims))])
    return level


def bell_draw(key, dims, spread, bound, cuts=(), kind=jnp.bfloat16):
    values = spread * jax.random.normal(key, dims, jnp.float32)
    if cuts:
        values = values * steps_of(key, dims, cuts, -0.22, 0.18)
    return jnp.clip(values, -bound, bound).astype(kind)


def setup_inputs(seed: int = 0) -> dict:
    key_of = jax.random.split(jax.random.key(seed), 5)
    return {
        "queries": bell_draw(key_of[0], (TOKENS, HEADS * HEAD_DIM), 1.0, 6.0, ((0, 8), (1, 4))),
        "keys_values": bell_draw(key_of[1], (TOKENS, 2 * HEAD_DIM), 1.0, 6.0, ((0, 8),)),
        "init_state": bell_draw(key_of[2], (HEAD_DIM, FEATURES), 8.0, 48.0, (), jnp.float32),
        "out_grad": bell_draw(key_of[3], (TOKENS, HEADS * HEAD_DIM), 1.0, 6.0, ((0, 8), (1, 4))),
    }


epsilon = 1e-06

def pair_tables(width):
    left_index, right_index = np.triu_indices(width)
    factor = np.where(left_index == right_index, 1.0, np.sqrt(2.0)) / np.sqrt(width)
    return (jnp.asarray(left_index, jnp.int32), jnp.asarray(right_index, jnp.int32), jnp.asarray(factor, jnp.float32))

def product(first, second, contract):
    return lax.dot_general(first.astype(jnp.float32), second.astype(jnp.float32), (contract, ((), ())), precision=lax.Precision.HIGHEST, preferred_element_type=jnp.float32)

def features(wide, tables):
    left_index, right_index, factor = tables
    return jnp.take(wide, left_index, axis=1) * jnp.take(wide, right_index, axis=1) * factor

def feature_grad(rows_in, upstream, tables):
    _, pullback = jax.vjp(lambda inner: features(inner, tables), rows_in.astype(jnp.float32))
    return pullback(lax.optimization_barrier(upstream).astype(jnp.float32))[0]

def head_pass(query, keys, values, start_low, grad, tables):
    width = query.shape[1]
    length = query.shape[0]
    qfeat = features(query.astype(jnp.float32), tables).astype(jnp.bfloat16)
    inter = product(qfeat, start_low, ((1,), (1,)))
    logits = product(query, keys, ((1,), (1,)))
    causal = lax.broadcasted_iota(jnp.int32, (length, length), 0) >= lax.broadcasted_iota(jnp.int32, (length, length), 1)
    weights = jnp.where(causal, logits * logits / width, 0.0).astype(jnp.bfloat16)
    numer = inter + product(weights, values, ((1,), (0,)))
    scale = lax.rsqrt(lax.optimization_barrier(jnp.mean(numer * numer, axis=1, keepdims=True)) + epsilon)
    normed = numer * scale
    upstream = grad.astype(jnp.float32)
    d_numer = (scale * (upstream - normed * lax.optimization_barrier(jnp.mean(upstream * normed, axis=1, keepdims=True)))).astype(jnp.bfloat16)
    d_qfeat = product(d_numer, start_low, ((1,), (0,))).astype(jnp.bfloat16)
    d_weights = product(d_numer, values, ((1,), (1,)))
    d_logits = jnp.where(causal, d_weights * logits * (2.0 / width), 0.0).astype(jnp.bfloat16)
    query_total = feature_grad(query, d_qfeat, tables) + product(d_logits, keys, ((1,), (0,)))
    key_local = product(d_logits, query, ((0,), (0,)))
    value_local = product(weights, d_numer, ((0,), (0,)))
    state_local = product(d_numer, qfeat, ((0,), (0,)))
    return (normed.astype(jnp.bfloat16), query_total.astype(jnp.bfloat16), key_local, value_local, state_local)

def reference(queries, keys_values, init_state, out_grad):
    tables = pair_tables(HEAD_DIM)
    count = TOKENS // GROUP
    query_blocks = queries.reshape(count, GROUP, HEADS * HEAD_DIM)
    kv_blocks = keys_values.reshape(count, GROUP, 2 * HEAD_DIM)
    grad_blocks = out_grad.reshape(count, GROUP, HEADS * HEAD_DIM)

    def block_update(block):
        kfeat = features(block[:, :HEAD_DIM].astype(jnp.float32), tables).astype(jnp.bfloat16)
        return product(block[:, HEAD_DIM:], kfeat, ((0,), (0,)))
    updates = lax.map(block_update, kv_blocks)
    before = jnp.concatenate([jnp.zeros_like(updates[:1]), jnp.cumsum(updates[:-1], axis=0)], axis=0)
    starts = (init_state[None] + before).astype(jnp.bfloat16)

    def block_pass(inputs):
        query_block, kv_block, grad_block, start_low = inputs
        keys = kv_block[:, :HEAD_DIM]
        values = kv_block[:, HEAD_DIM:]
        query_heads = query_block.reshape(GROUP, HEADS, HEAD_DIM).transpose(1, 0, 2)
        grad_heads = grad_block.reshape(GROUP, HEADS, HEAD_DIM).transpose(1, 0, 2)

        def one_head(pair):
            return head_pass(pair[0], keys, values, start_low, pair[1], tables)
        normed, qgrad, key_part, value_part, state_part = lax.map(one_head, (query_heads, grad_heads))
        return (normed.transpose(1, 0, 2).reshape(GROUP, HEADS * HEAD_DIM), qgrad.transpose(1, 0, 2).reshape(GROUP, HEADS * HEAD_DIM), lax.optimization_barrier(jnp.sum(key_part, axis=0)), lax.optimization_barrier(jnp.sum(value_part, axis=0)), lax.optimization_barrier(jnp.sum(state_part, axis=0)))
    attended, query_grad, key_local, value_local, state_grads = lax.map(block_pass, (query_blocks, kv_blocks, grad_blocks, starts))
    suffix = jnp.cumsum(state_grads[::-1], axis=0)[::-1]
    later = jnp.concatenate([suffix[1:], jnp.zeros_like(suffix[:1])], axis=0).astype(jnp.bfloat16)
    init_grad = suffix[0]

    def key_pass(inputs):
        kv_block, later_low = inputs
        keys = kv_block[:, :HEAD_DIM]
        values = kv_block[:, HEAD_DIM:]
        kfeat = features(keys.astype(jnp.float32), tables).astype(jnp.bfloat16)
        value_state = product(kfeat, later_low, ((1,), (1,)))
        d_kfeat = product(values, later_low, ((1,), (0,))).astype(jnp.bfloat16)
        key_state = feature_grad(keys, d_kfeat, tables)
        return (key_state, value_state)
    key_state, value_state = lax.map(key_pass, (kv_blocks, later))
    kv_grad = jnp.concatenate([key_local + key_state, value_local + value_state], axis=2)
    return (attended.reshape(TOKENS, HEADS * HEAD_DIM), query_grad.reshape(TOKENS, HEADS * HEAD_DIM), kv_grad.reshape(TOKENS, 2 * HEAD_DIM).astype(jnp.float32), init_grad)
```

```python
import functools

import jax
import jax.numpy as jnp
import numpy as np
from jax import lax
from jax.experimental import pallas as pl
from jax.experimental.pallas import tpu as pltpu
from jax.sharding import PartitionSpec as P

HEAD_DIM = 64
GROUP = 1024
EPS = 1e-06
CHUNK = 256
MESH = pl.DeviceIdType.MESH
F32, BF16 = jnp.float32, jnp.bfloat16


def padded_layout(width):
    starts, at = [], 0
    for a in range(width):
        starts.append(at)
        at += width - a // 8 * 8
    return starts, at


STARTS, PADDED = padded_layout(HEAD_DIM)
CANON = [a * HEAD_DIM - a * (a - 1) // 2 for a in range(HEAD_DIM)]


def dot(first, second, contract=((1,), (0,))):
    return lax.dot_general(first, second, (contract, ((), ())), preferred_element_type=F32)


def edge_weights(cols):
    row = lax.broadcasted_iota(jnp.int32, (8, cols), 0)
    return [
        jnp.where(row < m, 0.0, jnp.where(row == m, float(np.sqrt(0.5)), 1.0)).astype(F32)
        for m in range(8)
    ]


def write_features(x_ref, xs_ref, f_ref, cols):
    edges = edge_weights(cols)
    for a in range(0, HEAD_DIM, 2):
        base = a // 8 * 8
        parts = []
        for c in (a, a + 1):
            prod = x_ref[c : c + 1, :] * xs_ref[base:, :]
            parts.append(prod[:8] * edges[c % 8])
            if base + 8 < HEAD_DIM:
                parts.append(prod[8:])
        at = STARTS[a]
        f_ref[at : at + 2 * (HEAD_DIM - base), :] = jnp.concatenate(parts, axis=0).astype(BF16)


def feature_grad(xs_ref, df_ref, row_ref, cols):
    edges = edge_weights(cols)
    tiles = HEAD_DIM // 8
    acc = [jnp.zeros((8, cols), F32) for _ in range(tiles)]
    for a in range(HEAD_DIM):
        first = a // 8
        xa = jnp.broadcast_to(xs_ref[a : a + 1, :], (8, cols))
        total = None
        for t in range(first, tiles):
            at = STARTS[a] + (t - first) * 8
            part = df_ref[at : at + 8, :]
            if t == first:
                part = part * edges[a % 8]
            acc[t] = acc[t] + part * xa
            term = part * xs_ref[t * 8 : t * 8 + 8, :]
            total = term if total is None else total + term
        row_ref[a : a + 1, :] = jnp.sum(total, axis=0, keepdims=True)
    return jnp.concatenate(acc, axis=0) + row_ref[...]


def scaled(x):
    return x * float(np.sqrt(2.0 / HEAD_DIM))


def prepare_kernel(rows, init_ref, kv_ref, initp_ref, u_ref, padt, kvt, xs, f):
    h = lax.axis_index("head")
    tokens = kv_ref.shape[0]
    padt[...] = jnp.zeros_like(padt)
    for a in range(HEAD_DIM):
        at = STARTS[a] + a % 8
        padt[at : at + HEAD_DIM - a, :] = init_ref[CANON[a] : CANON[a] + HEAD_DIM - a, :]
    initp_ref[...] = padt[...].T
    kvt[...] = kv_ref[...].astype(F32).T
    vals = kvt[pl.ds(pl.multiple_of(HEAD_DIM + h * rows, 8), rows), :].astype(BF16)
    for c in range(tokens // CHUNK):
        at = slice(c * CHUNK, (c + 1) * CHUNK)
        x = kvt.at[:HEAD_DIM, at]
        xs[...] = scaled(x[...])
        write_features(x, xs, f, CHUNK)
        part = dot(vals[:, at], f[...], ((1,), (1,)))
        if c == 0:
            u_ref[...] = part
        else:
            u_ref[...] += part


def head_kernel(
    q_ref, kv_ref, initp_ref, carry_ref, og_ref,
    att_ref, qg_ref, kvl_ref, sg_ref,
    qt, ogt, attt, qgt, start, startt, keys, vals, kt, vt, f, df, x, xs, row,
):
    tokens = q_ref.shape[0]
    heads = q_ref.shape[1] // HEAD_DIM
    qt[...] = q_ref[...].astype(F32).T
    ogt[...] = og_ref[...].astype(F32).T
    kvt = kv_ref[...].astype(F32).T
    kt[...] = kvt[:HEAD_DIM].astype(BF16)
    vt[...] = kvt[HEAD_DIM:].astype(BF16)
    keys[...] = kv_ref[:, :HEAD_DIM]
    vals[...] = kv_ref[:, HEAD_DIM:]
    first = initp_ref[...] + carry_ref[...]
    start[...] = first.astype(BF16)
    startt[...] = first.T.astype(BF16)
    kvl_ref[...] = jnp.zeros_like(kvl_ref)
    sg_ref[...] = jnp.zeros_like(sg_ref)
    causal = lax.broadcasted_iota(jnp.int32, (CHUNK, CHUNK), 0) <= lax.broadcasted_iota(
        jnp.int32, (CHUNK, CHUNK), 1
    )

    def masked(full):
        n = full.shape[0]
        last = jnp.where(causal, full[n - CHUNK :], 0.0)
        if n == CHUNK:
            return last.astype(BF16)
        return jnp.concatenate([full[: n - CHUNK], last], axis=0).astype(BF16)

    for c in range(tokens // CHUNK):
        n = (c + 1) * CHUNK
        at = slice(c * CHUNK, n)

        def one_head(h, _):
            here = pl.ds(pl.multiple_of(h * HEAD_DIM, HEAD_DIM), HEAD_DIM)
            query = qt[here, at]
            x[...] = query
            xs[...] = scaled(query)
            write_features(x, xs, f, CHUNK)
            low = query.astype(BF16)
            logits = dot(keys[:n], low)
            weights = masked(logits * logits * (1.0 / HEAD_DIM))
            numer = dot(start[...], f[...]) + dot(vt[:, :n], weights)
            scale = lax.rsqrt(jnp.mean(numer * numer, axis=0, keepdims=True) + EPS)
            normed = numer * scale
            up = ogt[here, at]
            attt[here, at] = normed
            dn = (scale * (up - normed * jnp.mean(up * normed, axis=0, keepdims=True))).astype(BF16)
            df[...] = dot(startt[...], dn)
            dw = dot(vals[:n], dn)
            dl = masked(dw * logits * (2.0 / HEAD_DIM))
            qgt[here, at] = dot(kt[:, :n], dl) + feature_grad(xs, df, row, CHUNK)
            kvl_ref[:n, :HEAD_DIM] += dot(dl, low, ((1,), (1,)))
            kvl_ref[:n, HEAD_DIM:] += dot(weights, dn, ((1,), (1,)))
            sg_ref[...] += dot(dn, f[...], ((1,), (1,)))
            return 0

        lax.fori_loop(0, heads, one_head, 0)
    att_ref[...] = attt[...].T.astype(BF16)
    qg_ref[...] = qgt[...].T.astype(BF16)


def peers(ns, nh):
    s, h = lax.axis_index("seq"), lax.axis_index("head")
    groups = ns // 2
    g, p = s // 2, s % 2
    partner = (s + 1 - 2 * p, h)
    ring = [(lax.rem(g + k, groups) * 2 + p, h) for k in range(1, groups)]
    across = [(s, lax.rem(h + k, nh)) for k in range(1, nh)]
    return s, h, g, p, partner, ring, across


def greet(devices):
    barrier = pltpu.get_barrier_semaphore()
    for device in devices:
        pl.semaphore_signal(barrier, inc=1, device_id=device, device_id_type=MESH)
    pl.semaphore_wait(barrier, len(devices))


def remote(src, dst, sends, recvs, k, device):
    return pltpu.make_async_remote_copy(
        src_ref=src, dst_ref=dst, send_sem=sends.at[k], recv_sem=recvs.at[k],
        device_id=device, device_id_type=MESH,
    )


def prefix_kernel(ns, nh, u_ref, out_ref, pair, both, got, pre, ps, pr, rs, rr, hs, hr):
    rows = u_ref.shape[0]
    s, h, g, p, partner, ring, across = peers(ns, nh)
    greet([partner] + ring + across)
    swap = remote(u_ref, pair, ps, pr, 0, partner)
    swap.start()
    swap.wait()
    both[...] = u_ref[...] + pair[...]
    moves = [remote(both, got.at[k], rs, rr, k, ring[k]) for k in range(len(ring))]
    for k, move in enumerate(moves):
        @pl.when(g + k + 1 < ns // 2)
        def _(move=move):
            move.start()
    pre[...] = jnp.where(p == 1, pair[...], 0.0)
    for k, move in enumerate(moves):
        @pl.when(g - k - 1 >= 0)
        def _(move=move, k=k):
            move.wait_recv()
            pre[...] += got[k]
    here = out_ref.at[pl.ds(pl.multiple_of(h * rows, 8), rows), :]
    spread = [remote(pre, here, hs, hr, k, across[k]) for k in range(len(across))]
    for copy in spread:
        copy.start()
    here[...] = pre[...]
    for k, move in enumerate(moves):
        @pl.when(g + k + 1 < ns // 2)
        def _(move=move):
            move.wait_send()
    for copy in spread:
        copy.wait()


def suffix_kernel(
    ns, nh, sg_ref, kvl_ref, later_ref, total_ref, kvq_ref,
    parts, kvparts, own, pair, both, got, late, tot,
    ss, sr, ks, kr, ps, pr, rs, rr, hs, hr, ts, tr,
):
    rows = sg_ref.shape[0] // nh
    quarter = kvl_ref.shape[0] // nh
    s, h, g, p, partner, ring, across = peers(ns, nh)
    greet([partner] + ring + across)
    scatter, kvscatter = [], []
    for k in range(nh - 1):
        to = lax.rem(h + k + 1, nh)
        src = sg_ref.at[pl.ds(pl.multiple_of(to * rows, 8), rows), :]
        scatter.append(remote(src, parts.at[k], ss, sr, k, across[k]))
    for copy in scatter:
        copy.start()
    for k in range(nh - 1):
        to = lax.rem(h + k + 1, nh)
        src = kvl_ref.at[pl.ds(pl.multiple_of(to * quarter, 8), quarter), :]
        kvscatter.append(remote(src, kvparts.at[k], ks, kr, k, across[k]))
    own[...] = sg_ref[pl.ds(pl.multiple_of(h * rows, 8), rows), :]
    for k, copy in enumerate(scatter):
        copy.wait()
        own[...] += parts[k]
    swap = remote(own, pair, ps, pr, 0, partner)
    swap.start()
    for copy in kvscatter:
        copy.start()
    swap.wait()
    both[...] = own[...] + pair[...]
    moves = [remote(both, got.at[k], rs, rr, k, ring[k]) for k in range(len(ring))]
    for move in moves:
        move.start()
    kvsum = kvl_ref[pl.ds(pl.multiple_of(h * quarter, 8), quarter), :]
    for k, copy in enumerate(kvscatter):
        copy.wait()
        kvsum = kvsum + kvparts[k]
    kvq_ref[...] = kvsum
    late[...] = jnp.where(p == 0, pair[...], 0.0)
    tot[...] = both[...]
    for k, move in enumerate(moves):
        move.wait_recv()
        tot[...] += got[k]
        late[...] += jnp.where(k + 1 > g, got[k], 0.0)
    at = pl.ds(pl.multiple_of(h * rows, 8), rows)
    spread = [remote(late, later_ref.at[at, :], hs, hr, k, across[k]) for k in range(nh - 1)]
    spread += [remote(tot, total_ref.at[at, :], ts, tr, k, across[k]) for k in range(nh - 1)]
    for copy in spread:
        copy.start()
    later_ref[at, :] = late[...]
    total_ref[at, :] = tot[...]
    for move in moves:
        move.wait_send()
    for copy in spread:
        copy.wait()


def key_kernel(kv_ref, later_ref, kvq_ref, out_ref, kvt, low, lowt, f, df, xs, row, gt):
    h = lax.axis_index("head")
    quarter = kvq_ref.shape[0]
    block = kv_ref[pl.ds(pl.multiple_of(h * quarter, 16), quarter), :]
    kvt[...] = block.astype(F32).T
    low[...] = later_ref[...].astype(BF16)
    lowt[...] = later_ref[...].T.astype(BF16)
    x = kvt.at[:HEAD_DIM, :]
    xs[...] = scaled(x[...])
    write_features(x, xs, f, quarter)
    gt[HEAD_DIM:, :] = dot(low[...], f[...])
    df[...] = dot(lowt[...], kvt[HEAD_DIM:, :].astype(BF16))
    gt[:HEAD_DIM, :] = feature_grad(xs, df, row, quarter)
    out_ref[...] = kvq_ref[...] + gt[...].T


def finish_kernel(ns, nh, part_ref, total_ref, kv_ref, init_ref, padt, canon, hs, hr):
    quarter = part_ref.shape[0]
    s, h, g, p, partner, ring, across = peers(ns, nh)
    greet(across)
    here = kv_ref.at[pl.ds(pl.multiple_of(h * quarter, 8), quarter), :]
    spread = [remote(part_ref, here, hs, hr, k, across[k]) for k in range(nh - 1)]
    for copy in spread:
        copy.start()
    here[...] = part_ref[...]
    padt[...] = total_ref[...].T
    for a in range(HEAD_DIM):
        at = STARTS[a] + a % 8
        canon[CANON[a] : CANON[a] + HEAD_DIM - a, :] = padt[at : at + HEAD_DIM - a, :]
    wide = init_ref.shape[0]
    init_ref[...] = canon[pl.ds(pl.multiple_of(h * wide, 8), wide), :]
    for copy in spread:
        copy.wait()


def call(kernel, outs, scratch, ins, collective=None):
    params = dict(vmem_limit_bytes=60 * 1024 * 1024)
    if collective is not None:
        params.update(collective_id=collective, has_side_effects=True)
    vmem = pl.BlockSpec(memory_space=pltpu.VMEM)
    return pl.pallas_call(
        kernel,
        out_shape=tuple(jax.ShapeDtypeStruct(shape, dtype) for shape, dtype in outs),
        in_specs=[vmem] * len(ins),
        out_specs=tuple(vmem for _ in outs),
        scratch_shapes=scratch,
        compiler_params=pltpu.CompilerParams(**params),
    )(*ins)


def per_device(ns, nh, queries, keys_values, init_state, out_grad):
    tokens, wide = queries.shape
    assert tokens == GROUP and ns % 2 == 0
    features = init_state.shape[1]
    rows, quarter = HEAD_DIM // nh, tokens // nh
    groups = ns // 2
    V, D = pltpu.VMEM, pltpu.SemaphoreType.DMA

    initp, u = call(
        functools.partial(prepare_kernel, rows),
        [((HEAD_DIM, PADDED), F32), ((rows, PADDED), F32)],
        [V((PADDED, HEAD_DIM), F32), V((2 * HEAD_DIM, tokens), F32),
         V((HEAD_DIM, CHUNK), F32), V((PADDED, CHUNK), BF16)],
        (init_state.T, keys_values),
    )
    part = (rows, PADDED)
    (carry,) = call(
        functools.partial(prefix_kernel, ns, nh),
        [((HEAD_DIM, PADDED), F32)],
        [V(part, F32), V(part, F32), V((groups - 1,) + part, F32), V(part, F32),
         D((1,)), D((1,)), D((groups - 1,)), D((groups - 1,)), D((nh - 1,)), D((nh - 1,))],
        (u,), 1,
    )
    attended, query_grad, kvl, sg = call(
        head_kernel,
        [((tokens, wide), BF16), ((tokens, wide), BF16),
         ((tokens, 2 * HEAD_DIM), F32), ((HEAD_DIM, PADDED), F32)],
        [V((wide, tokens), F32)] * 4
        + [V((HEAD_DIM, PADDED), BF16), V((PADDED, HEAD_DIM), BF16)]
        + [V((tokens, HEAD_DIM), BF16)] * 2 + [V((HEAD_DIM, tokens), BF16)] * 2
        + [V((PADDED, CHUNK), BF16), V((PADDED, CHUNK), F32)]
        + [V((HEAD_DIM, CHUNK), F32)] * 3,
        (queries, keys_values, initp, carry, out_grad),
    )
    later, total, kvq = call(
        functools.partial(suffix_kernel, ns, nh),
        [((HEAD_DIM, PADDED), F32), ((HEAD_DIM, PADDED), F32), ((quarter, 2 * HEAD_DIM), F32)],
        [V((nh - 1,) + part, F32), V((nh - 1, quarter, 2 * HEAD_DIM), F32),
         V(part, F32), V(part, F32), V(part, F32), V((groups - 1,) + part, F32),
         V(part, F32), V(part, F32)]
        + [D((nh - 1,))] * 4 + [D((1,))] * 2 + [D((groups - 1,))] * 2 + [D((nh - 1,))] * 4,
        (sg, kvl), 2,
    )
    (mine,) = call(
        key_kernel,
        [((quarter, 2 * HEAD_DIM), F32)],
        [V((2 * HEAD_DIM, quarter), F32), V((HEAD_DIM, PADDED), BF16),
         V((PADDED, HEAD_DIM), BF16), V((PADDED, quarter), BF16), V((PADDED, quarter), F32),
         V((HEAD_DIM, quarter), F32), V((HEAD_DIM, quarter), F32), V((2 * HEAD_DIM, quarter), F32)],
        (keys_values, later, kvq),
    )
    kv_grad, init_grad = call(
        functools.partial(finish_kernel, ns, nh),
        [((tokens, 2 * HEAD_DIM), F32), ((features // nh, HEAD_DIM), F32)],
        [V((PADDED, HEAD_DIM), F32), V((features, HEAD_DIM), F32), D((nh - 1,)), D((nh - 1,))],
        (mine, total), 3,
    )
    return (attended, query_grad, kv_grad, init_grad.T)


def solution(mesh):
    ns, nh = mesh.shape["seq"], mesh.shape["head"]
    return jax.shard_map(
        functools.partial(per_device, ns, nh),
        mesh=mesh,
        in_specs=(P("seq", "head"), P("seq", None), P(), P("seq", "head")),
        out_specs=(P("seq", "head"), P("seq", "head"), P("seq", None), P(None, "head")),
        check_vma=False,
    )
```

```python
import functools

import jax
import jax.numpy as jnp
import numpy as np
from jax import lax
from jax.experimental import pallas as pl
from jax.experimental.pallas import tpu as pltpu
from jax.sharding import PartitionSpec as P

HEAD_DIM = 64
GROUP = 1024
EPS = 1e-06
CHUNK = 256
MESH = pl.DeviceIdType.MESH
F32, BF16 = jnp.float32, jnp.bfloat16


def padded_layout(width):
    starts, at = [], 0
    for a in range(width):
        starts.append(at)
        at += width - a // 8 * 8
    return starts, at


STARTS, PADDED = padded_layout(HEAD_DIM)
CANON = [a * HEAD_DIM - a * (a - 1) // 2 for a in range(HEAD_DIM)]


def dot(first, second, contract=((1,), (0,))):
    return lax.dot_general(first, second, (contract, ((), ())), preferred_element_type=F32)


def edge_weights(cols):
    row = lax.broadcasted_iota(jnp.int32, (8, cols), 0)
    return [
        jnp.where(row < m, 0.0, jnp.where(row == m, float(np.sqrt(0.5)), 1.0)).astype(F32)
        for m in range(8)
    ]


def write_features(x_ref, xs_ref, f_ref, cols):
    edges = edge_weights(cols)
    for a in range(0, HEAD_DIM, 2):
        base = a // 8 * 8
        parts = []
        for c in (a, a + 1):
            prod = x_ref[c : c + 1, :] * xs_ref[base:, :]
            parts.append(prod[:8] * edges[c % 8])
            if base + 8 < HEAD_DIM:
                parts.append(prod[8:])
        at = STARTS[a]
        f_ref[at : at + 2 * (HEAD_DIM - base), :] = jnp.concatenate(parts, axis=0).astype(BF16)


def feature_grad(xs_ref, df_ref, row_ref, cols):
    edges = edge_weights(cols)
    tiles = HEAD_DIM // 8
    acc = [jnp.zeros((8, cols), F32) for _ in range(tiles)]
    for a in range(HEAD_DIM):
        first = a // 8
        xa = jnp.broadcast_to(xs_ref[a : a + 1, :], (8, cols))
        total = None
        for t in range(first, tiles):
            at = STARTS[a] + (t - first) * 8
            part = df_ref[at : at + 8, :]
            if t == first:
                part = part * edges[a % 8]
            acc[t] = acc[t] + part * xa
            term = part * xs_ref[t * 8 : t * 8 + 8, :]
            total = term if total is None else total + term
        row_ref[a : a + 1, :] = jnp.sum(total, axis=0, keepdims=True)
    return jnp.concatenate(acc, axis=0) + row_ref[...]


def scaled(x):
    return x * float(np.sqrt(2.0 / HEAD_DIM))


def prepare_kernel(rows, init_ref, kv_ref, initp_ref, u_ref, wide, tall, padt, kvt, xs, f):
    h = lax.axis_index("head")
    tokens = kv_ref.shape[0]
    features = init_ref.shape[1]
    padt[...] = jnp.zeros_like(padt)
    wide[:, features // 128 * 128 :] = jnp.zeros_like(wide[:, features // 128 * 128 :])
    wide[:, :features] = init_ref[...]
    tall[...] = wide[...].T
    for a in range(HEAD_DIM):
        at = STARTS[a] + a % 8
        padt[at : at + HEAD_DIM - a, :] = tall[CANON[a] : CANON[a] + HEAD_DIM - a, :]
    initp_ref[...] = padt[...].T
    kvt[...] = kv_ref[...].astype(F32).T
    vals = kvt[pl.ds(pl.multiple_of(HEAD_DIM + h * rows, 8), rows), :].astype(BF16)
    for c in range(tokens // CHUNK):
        at = slice(c * CHUNK, (c + 1) * CHUNK)
        x = kvt.at[:HEAD_DIM, at]
        xs[...] = scaled(x[...])
        write_features(x, xs, f, CHUNK)
        part = dot(vals[:, at], f[...], ((1,), (1,)))
        if c == 0:
            u_ref[...] = part
        else:
            u_ref[...] += part


def head_kernel(
    q_ref, kv_ref, initp_ref, carry_ref, og_ref,
    att_ref, qg_ref, kvl_ref, sg_ref,
    qt, ogt, attt, qgt, start, startt, keys, vals, kt, vt, f, df, x, xs, row,
):
    tokens = q_ref.shape[0]
    heads = q_ref.shape[1] // HEAD_DIM
    qt[...] = q_ref[...].astype(F32).T
    ogt[...] = og_ref[...].astype(F32).T
    kvt = kv_ref[...].astype(F32).T
    kt[...] = kvt[:HEAD_DIM].astype(BF16)
    vt[...] = kvt[HEAD_DIM:].astype(BF16)
    keys[...] = kv_ref[:, :HEAD_DIM]
    vals[...] = kv_ref[:, HEAD_DIM:]
    first = initp_ref[...] + carry_ref[...]
    start[...] = first.astype(BF16)
    startt[...] = first.T.astype(BF16)
    kvl_ref[...] = jnp.zeros_like(kvl_ref)
    sg_ref[...] = jnp.zeros_like(sg_ref)
    causal = lax.broadcasted_iota(jnp.int32, (CHUNK, CHUNK), 0) <= lax.broadcasted_iota(
        jnp.int32, (CHUNK, CHUNK), 1
    )

    def masked(full):
        n = full.shape[0]
        last = jnp.where(causal, full[n - CHUNK :], 0.0)
        if n == CHUNK:
            return last.astype(BF16)
        return jnp.concatenate([full[: n - CHUNK], last], axis=0).astype(BF16)

    for c in range(tokens // CHUNK):
        n = (c + 1) * CHUNK
        at = slice(c * CHUNK, n)

        def one_head(h, _):
            here = pl.ds(pl.multiple_of(h * HEAD_DIM, HEAD_DIM), HEAD_DIM)
            query = qt[here, at]
            x[...] = query
            xs[...] = scaled(query)
            write_features(x, xs, f, CHUNK)
            low = query.astype(BF16)
            logits = dot(keys[:n], low)
            weights = masked(logits * logits * (1.0 / HEAD_DIM))
            numer = dot(start[...], f[...]) + dot(vt[:, :n], weights)
            scale = lax.rsqrt(jnp.mean(numer * numer, axis=0, keepdims=True) + EPS)
            normed = numer * scale
            up = ogt[here, at]
            attt[here, at] = normed
            dn = (scale * (up - normed * jnp.mean(up * normed, axis=0, keepdims=True))).astype(BF16)
            df[...] = dot(startt[...], dn)
            dw = dot(vals[:n], dn)
            dl = masked(dw * logits * (2.0 / HEAD_DIM))
            qgt[here, at] = dot(kt[:, :n], dl) + feature_grad(xs, df, row, CHUNK)
            kvl_ref[:n, :HEAD_DIM] += dot(dl, low, ((1,), (1,)))
            kvl_ref[:n, HEAD_DIM:] += dot(weights, dn, ((1,), (1,)))
            sg_ref[...] += dot(dn, f[...], ((1,), (1,)))
            return 0

        lax.fori_loop(0, heads, one_head, 0)
    att_ref[...] = attt[...].T.astype(BF16)
    qg_ref[...] = qgt[...].T.astype(BF16)


def places(ns, nh):
    s, h = lax.axis_index("seq"), lax.axis_index("head")
    groups = ns // 2
    g, p = s // 2, s % 2
    beside = h + 1 - 2 * (h % 2)
    partner = (s + 1 - 2 * p, h)
    ring = [(lax.rem(g + k, groups) * 2 + p, h) for k in range(1, groups)]
    across = [(s, lax.rem(h + k, nh)) for k in range(1, nh)]
    return s, h, g, p, beside, partner, ring, across


def greet(devices):
    barrier = pltpu.get_barrier_semaphore()
    for device in devices:
        pl.semaphore_signal(barrier, inc=1, device_id=device, device_id_type=MESH)
    pl.semaphore_wait(barrier, len(devices))


def block(index, size):
    return pl.ds(pl.multiple_of(index * size, 8), size)


class Links:
    def __init__(self, sends, recvs):
        self.sends, self.recvs, self.used = sends, recvs, 0

    def copy(self, src, dst, device):
        k = self.used
        self.used += 1
        return pltpu.make_async_remote_copy(
            src_ref=src, dst_ref=dst, send_sem=self.sends.at[k], recv_sem=self.recvs.at[k],
            device_id=device, device_id_type=MESH,
        )


def gather_copies(links, nh, s, h, beside, src, out, size, spot):
    far = []
    for k in range(2, nh, 2):
        to = lax.rem(h + k, nh)
        first = links.copy(src, out.at[spot(h)], (s, to))
        came = out.at[spot(lax.rem(h + nh - k, nh))]
        far.append((first, links.copy(came, came, (s, beside))))
    near = links.copy(src, out.at[spot(h)], (s, beside))
    return far, near


def spread_piece(links, nh, s, h, beside, out, half, slot):
    spot = lambda owner: block(owner * 2 + slot, half)
    return gather_copies(links, nh, s, h, beside, out.at[spot(h)], out, half, spot)


def start_gather(gather):
    far, near = gather
    for first, _ in far:
        first.start()
    near.start()


def forward_gather(gather):
    for first, second in gather[0]:
        first.wait_recv()
        second.start()


def finish_gather(gather):
    far, near = gather
    for first, second in far:
        first.wait_send()
        second.wait()
    near.wait()


def prefix_kernel(ns, nh, u_ref, out_ref, pair, both, got, mate, sends, recvs):
    half = u_ref.shape[0] // 2
    groups = ns // 2
    s, h, g, p, beside, partner, ring, across = places(ns, nh)
    links = Links(sends, recvs)
    greet([partner] + ring + across)
    swap = links.copy(u_ref.at[block(1 - p, half), :], pair, partner)
    swap.start()
    swap.wait()
    mine = u_ref[block(p, half), :]
    both[...] = mine + pair[...]
    moves = [links.copy(both, got.at[k], ring[k]) for k in range(groups - 1)]
    for k, move in enumerate(moves):
        @pl.when(g + k + 1 < groups)
        def _(move=move):
            move.start()
    ours = block(h * 2 + p, half)
    theirs = block(h * 2 + 1 - p, half)
    out_ref[ours, :] = jnp.where(p == 1, pair[...], 0.0)
    mate[...] = jnp.where(p == 0, mine, 0.0)
    for k, move in enumerate(moves):
        @pl.when(g - k - 1 >= 0)
        def _(move=move, k=k):
            move.wait_recv()
            out_ref[ours, :] += got[k]
            mate[...] += got[k]
    back = links.copy(mate, out_ref.at[ours, :], partner)
    back.start()
    own_half = spread_piece(links, nh, s, h, beside, out_ref, half, p)
    start_gather(own_half)
    other_half = spread_piece(links, nh, s, h, beside, out_ref, half, 1 - p)
    back.wait_recv()
    start_gather(other_half)
    forward_gather(own_half)
    forward_gather(other_half)
    for k, move in enumerate(moves):
        @pl.when(g + k + 1 < groups)
        def _(move=move):
            move.wait_send()
    back.wait_send()
    finish_gather(own_half)
    finish_gather(other_half)


def suffix_kernel(
    ns, nh, sg_ref, kvl_ref, later_ref, total_ref, kvq_ref,
    near, far, mid, kvparts, own, pair, both, got, mate, tot, sends, recvs,
):
    rows = sg_ref.shape[0] // nh
    half = rows // 2
    groups = ns // 2
    quarter = kvl_ref.shape[0] // nh
    s, h, g, p, beside, partner, ring, across = places(ns, nh)
    links = Links(sends, recvs)
    greet([partner] + ring + across)
    evens = range(2, nh + 1, 2)
    first = []
    for i, k in enumerate(evens):
        src = sg_ref.at[block(lax.rem(beside + k, nh), rows), :]
        first.append(links.copy(src, near.at[i], (s, beside)))
    for copy in first:
        copy.start()
    second = []
    for i, k in enumerate(evens):
        first[i].wait_recv()
        summed = sg_ref[block(lax.rem(h + k, nh), rows), :] + near[i]
        if k == nh:
            own[...] = summed
        else:
            mid[i] = summed
            second.append(links.copy(mid.at[i], far.at[i], (s, lax.rem(h + k, nh))))
            second[-1].start()
    kvscatter = []
    for k in range(nh - 1):
        src = kvl_ref.at[block(lax.rem(h + k + 1, nh), quarter), :]
        kvscatter.append(links.copy(src, kvparts.at[k], across[k]))
    for i, copy in enumerate(second):
        copy.wait_recv()
        own[...] += far[i]
    swap = links.copy(own.at[block(1 - p, half), :], pair, partner)
    swap.start()
    for copy in kvscatter:
        copy.start()
    swap.wait()
    mine = own[block(p, half), :]
    both[...] = mine + pair[...]
    moves = [links.copy(both, got.at[k], ring[k]) for k in range(groups - 1)]
    for move in moves:
        move.start()
    ours = block(h * 2 + p, half)
    theirs = block(h * 2 + 1 - p, half)
    kvsum = kvl_ref[block(h, quarter), :]
    for k, copy in enumerate(kvscatter):
        copy.wait()
        kvsum = kvsum + kvparts[k]
    kvq_ref[...] = kvsum
    later = jnp.where(p == 0, pair[...], 0.0)
    mated = jnp.where(p == 1, mine, 0.0)
    whole = both[...]
    for k, move in enumerate(moves):
        move.wait_recv()
        whole = whole + got[k]
        after = jnp.where(k + 1 > g, got[k], 0.0)
        later = later + after
        mated = mated + after
    later_ref[ours, :] = later
    mate[...] = mated
    tot[...] = whole
    back = links.copy(mate, later_ref.at[ours, :], partner)
    back.start()
    own_half = spread_piece(links, nh, s, h, beside, later_ref, half, p)
    start_gather(own_half)
    total_swap = links.copy(tot, total_ref.at[block(p, half), :], partner)
    total_swap.start()
    other_half = spread_piece(links, nh, s, h, beside, later_ref, half, 1 - p)
    back.wait_recv()
    start_gather(other_half)
    total_ref[block(p, half), :] = tot[...]
    forward_gather(own_half)
    forward_gather(other_half)
    for copy in first + second + moves + [back]:
        copy.wait_send()
    total_swap.wait()
    finish_gather(own_half)
    finish_gather(other_half)


def key_kernel(kv_ref, later_ref, kvq_ref, out_ref, kvt, low, lowt, f, df, xs, row, gt):
    h = lax.axis_index("head")
    quarter = kvq_ref.shape[0]
    kvt[...] = kv_ref[pl.ds(pl.multiple_of(h * quarter, 16), quarter), :].astype(F32).T
    low[...] = later_ref[...].astype(BF16)
    lowt[...] = later_ref[...].T.astype(BF16)
    x = kvt.at[:HEAD_DIM, :]
    xs[...] = scaled(x[...])
    write_features(x, xs, f, quarter)
    gt[HEAD_DIM:, :] = dot(low[...], f[...])
    df[...] = dot(lowt[...], kvt[HEAD_DIM:, :].astype(BF16))
    gt[:HEAD_DIM, :] = feature_grad(xs, df, row, quarter)
    out_ref[...] = kvq_ref[...] + gt[...].T


def padded_column(c):
    a = max(a for a in range(HEAD_DIM) if CANON[a] <= c)
    return STARTS[a] + a % 8 + c - CANON[a]


def windows(features, nh):
    wide = features // nh
    ends = [(padded_column(k * wide), padded_column(k * wide + wide - 1)) for k in range(nh)]
    width = max(-(-(hi + 1) // 128) * 128 - lo // 128 * 128 for lo, hi in ends)
    return [min(lo // 128 * 128, PADDED - width) for lo, _ in ends], width


def window_at(starts, owner, nh):
    at = starts[0]
    for k in range(1, nh):
        at = at + (starts[k] - starts[k - 1]) * ((owner + nh - k) // nh)
    return at


def finish_kernel(
    ns, nh, starts, width, part_ref, total_ref, kv_ref, init_ref,
    win, padt, canon, flip, sends, recvs,
):
    quarter = part_ref.shape[0]
    rows = total_ref.shape[0]
    s, h, g, p, beside, partner, ring, across = places(ns, nh)
    links = Links(sends, recvs)
    greet(across)
    spot = lambda owner: block(owner, quarter)
    parts = gather_copies(links, nh, s, h, beside, part_ref, kv_ref, quarter, spot)
    start_gather(parts)
    moves = []
    for k in range(nh - 1):
        to = lax.rem(h + k + 1, nh)
        columns = pl.ds(pl.multiple_of(window_at(starts, to, nh), 128), width)
        move = links.copy(total_ref.at[:, columns], win.at[block(h, rows), :], across[k])
        move.start()
        moves.append(move)
    mine = pl.ds(pl.multiple_of(window_at(starts, h, nh), 128), width)
    win[block(h, rows), :] = total_ref[:, mine]
    kv_ref[spot(h), :] = part_ref[...]
    forward_gather(parts)
    for move in moves:
        move.wait()
    padt[pl.ds(pl.multiple_of(window_at(starts, h, nh), 128), width), :] = win[...].T
    for a in range(HEAD_DIM):
        at = STARTS[a] + a % 8
        canon[CANON[a] : CANON[a] + HEAD_DIM - a, :] = padt[at : at + HEAD_DIM - a, :]
    wide = init_ref.shape[1]
    flip[:wide, :] = canon[block(h, wide), :]
    init_ref[...] = flip[...].T[:, :wide]
    finish_gather(parts)


def call(kernel, outs, scratch, ins, collective=None):
    params = dict(vmem_limit_bytes=60 * 1024 * 1024)
    if collective is not None:
        params.update(collective_id=collective, has_side_effects=True)
    vmem = pl.BlockSpec(memory_space=pltpu.VMEM)
    return pl.pallas_call(
        kernel,
        out_shape=tuple(jax.ShapeDtypeStruct(shape, dtype) for shape, dtype in outs),
        in_specs=[vmem] * len(ins),
        out_specs=tuple(vmem for _ in outs),
        scratch_shapes=scratch,
        compiler_params=pltpu.CompilerParams(**params),
    )(*ins)


def per_device(ns, nh, queries, keys_values, init_state, out_grad):
    tokens, wide = queries.shape
    assert tokens == GROUP and ns % 2 == 0 and nh % 2 == 0
    features = init_state.shape[1]
    rows, quarter = HEAD_DIM // nh, tokens // nh
    groups = ns // 2
    V, D = pltpu.VMEM, pltpu.SemaphoreType.DMA

    even = -(-features // 128) * 128
    initp, u = call(
        functools.partial(prepare_kernel, rows),
        [((HEAD_DIM, PADDED), F32), ((rows, PADDED), F32)],
        [V((HEAD_DIM, even), F32), V((even, HEAD_DIM), F32),
         V((PADDED, HEAD_DIM), F32), V((2 * HEAD_DIM, tokens), F32),
         V((HEAD_DIM, CHUNK), F32), V((PADDED, CHUNK), BF16)],
        (init_state, keys_values),
    )
    part, piece = (rows, PADDED), (rows // 2, PADDED)
    gathers = nh - 1
    count = 2 + (groups - 1) + 2 * gathers
    (carry,) = call(
        functools.partial(prefix_kernel, ns, nh),
        [((HEAD_DIM, PADDED), F32)],
        [V(piece, F32), V(piece, F32), V((groups - 1,) + piece, F32), V(piece, F32),
         D((count,)), D((count,))],
        (u,), 1,
    )
    attended, query_grad, kvl, sg = call(
        head_kernel,
        [((tokens, wide), BF16), ((tokens, wide), BF16),
         ((tokens, 2 * HEAD_DIM), F32), ((HEAD_DIM, PADDED), F32)],
        [V((wide, tokens), F32)] * 4
        + [V((HEAD_DIM, PADDED), BF16), V((PADDED, HEAD_DIM), BF16)]
        + [V((tokens, HEAD_DIM), BF16)] * 2 + [V((HEAD_DIM, tokens), BF16)] * 2
        + [V((PADDED, CHUNK), BF16), V((PADDED, CHUNK), F32)]
        + [V((HEAD_DIM, CHUNK), F32)] * 3,
        (queries, keys_values, initp, carry, out_grad),
    )
    count = nh // 2 + (nh // 2 - 1) + (nh - 1) + 3 + (groups - 1) + 2 * gathers
    later, total, kvq = call(
        functools.partial(suffix_kernel, ns, nh),
        [((HEAD_DIM, PADDED), F32), (part, F32), ((quarter, 2 * HEAD_DIM), F32)],
        [V((nh // 2,) + part, F32)] * 3 + [V((nh - 1, quarter, 2 * HEAD_DIM), F32),
         V(part, F32), V(piece, F32), V(piece, F32), V((groups - 1,) + piece, F32),
         V(piece, F32), V(piece, F32), D((count,)), D((count,))],
        (sg, kvl), 2,
    )
    (mine,) = call(
        key_kernel,
        [((quarter, 2 * HEAD_DIM), F32)],
        [V((2 * HEAD_DIM, quarter), F32), V((HEAD_DIM, PADDED), BF16),
         V((PADDED, HEAD_DIM), BF16), V((PADDED, quarter), BF16), V((PADDED, quarter), F32),
         V((HEAD_DIM, quarter), F32), V((HEAD_DIM, quarter), F32), V((2 * HEAD_DIM, quarter), F32)],
        (keys_values, later, kvq),
    )
    starts, width = windows(features, nh)
    slice_width = features // nh
    count = gathers + nh - 1
    kv_grad, init_grad = call(
        functools.partial(finish_kernel, ns, nh, starts, width),
        [((tokens, 2 * HEAD_DIM), F32), ((HEAD_DIM, slice_width), F32)],
        [V((HEAD_DIM, width), F32), V((PADDED, HEAD_DIM), F32), V((features, HEAD_DIM), F32),
         V((-(-slice_width // 128) * 128, HEAD_DIM), F32), D((count,)), D((count,))],
        (mine, total), 3,
    )
    return (attended, query_grad, kv_grad, init_grad)


def solution(mesh):
    ns, nh = mesh.shape["seq"], mesh.shape["head"]
    return jax.shard_map(
        functools.partial(per_device, ns, nh),
        mesh=mesh,
        in_specs=(P("seq", "head"), P("seq", None), P(), P("seq", "head")),
        out_specs=(P("seq", "head"), P("seq", "head"), P("seq", None), P(None, "head")),
        check_vma=False,
    )
```

```python
import functools

import jax
import jax.numpy as jnp
import numpy as np
from jax import lax
from jax.experimental import pallas as pl
from jax.experimental.pallas import tpu as pltpu
from jax.sharding import PartitionSpec as P

HEAD_DIM = 64
GROUP = 1024
EPS = 1e-06
CHUNK = 256
MESH = pl.DeviceIdType.MESH
F32, BF16 = jnp.float32, jnp.bfloat16


def padded_layout(width):
    starts, at = [], 0
    for a in range(width):
        starts.append(at)
        at += width - a // 8 * 8
    return starts, at


STARTS, PADDED = padded_layout(HEAD_DIM)
CANON = [a * HEAD_DIM - a * (a - 1) // 2 for a in range(HEAD_DIM)]


def dot(first, second, contract=((1,), (0,))):
    return lax.dot_general(first, second, (contract, ((), ())), preferred_element_type=F32)


def edge_weights(cols):
    row = lax.broadcasted_iota(jnp.int32, (8, cols), 0)
    return [
        jnp.where(row < m, 0.0, jnp.where(row == m, float(np.sqrt(0.5)), 1.0)).astype(F32)
        for m in range(8)
    ]


def write_features(x_ref, xs_ref, f_ref, cols):
    edges = edge_weights(cols)
    for a in range(0, HEAD_DIM, 2):
        base = a // 8 * 8
        parts = []
        for c in (a, a + 1):
            prod = x_ref[c : c + 1, :] * xs_ref[base:, :]
            parts.append(prod[:8] * edges[c % 8])
            if base + 8 < HEAD_DIM:
                parts.append(prod[8:])
        at = STARTS[a]
        f_ref[at : at + 2 * (HEAD_DIM - base), :] = jnp.concatenate(parts, axis=0).astype(BF16)


def feature_grad(xs_ref, df_ref, row_ref, cols):
    edges = edge_weights(cols)
    tiles = HEAD_DIM // 8
    acc = [jnp.zeros((8, cols), F32) for _ in range(tiles)]
    for a in range(HEAD_DIM):
        first = a // 8
        xa = jnp.broadcast_to(xs_ref[a : a + 1, :], (8, cols))
        total = None
        for t in range(first, tiles):
            at = STARTS[a] + (t - first) * 8
            part = df_ref[at : at + 8, :]
            if t == first:
                part = part * edges[a % 8]
            acc[t] = acc[t] + part * xa
            term = part * xs_ref[t * 8 : t * 8 + 8, :]
            total = term if total is None else total + term
        row_ref[a : a + 1, :] = jnp.sum(total, axis=0, keepdims=True)
    return jnp.concatenate(acc, axis=0) + row_ref[...]


def scaled(x):
    return x * float(np.sqrt(2.0 / HEAD_DIM))


def places(ns, nh):
    s, h = lax.axis_index("seq"), lax.axis_index("head")
    groups = ns // 2
    g, p = s // 2, s % 2
    beside = h + 1 - 2 * (h % 2)
    partner = (s + 1 - 2 * p, h)
    ring = [(lax.rem(g + k, groups) * 2 + p, h) for k in range(1, groups)]
    across = [(s, lax.rem(h + k, nh)) for k in range(1, nh)]
    return s, h, g, p, beside, partner, ring, across


def block(index, size):
    return pl.ds(pl.multiple_of(index * size, 8), size)


class Links:
    def __init__(self, sends, recvs):
        self.sends, self.recvs, self.used = sends, recvs, 0

    def copy(self, src, dst, device):
        k = self.used
        self.used += 1
        return pltpu.make_async_remote_copy(
            src_ref=src, dst_ref=dst, send_sem=self.sends.at[k], recv_sem=self.recvs.at[k],
            device_id=device, device_id_type=MESH,
        )


def gather_copies(links, nh, s, h, beside, src, out, size, spot):
    far = []
    for k in range(2, nh, 2):
        to = lax.rem(h + k, nh)
        first = links.copy(src, out.at[spot(h)], (s, to))
        came = out.at[spot(lax.rem(h + nh - k, nh))]
        far.append((first, links.copy(came, came, (s, beside))))
    near = links.copy(src, out.at[spot(h)], (s, beside))
    return far, near


def spread_piece(links, nh, s, h, beside, out, half, slot):
    spot = lambda owner: block(owner * 2 + slot, half)
    return gather_copies(links, nh, s, h, beside, out.at[spot(h)], out, half, spot)


def start_gather(gather):
    far, near = gather
    for first, _ in far:
        first.start()
    near.start()


def forward_gather(gather):
    for first, second in gather[0]:
        first.wait_recv()
        second.start()


def finish_gather(gather):
    far, near = gather
    for first, second in far:
        first.wait_send()
        second.wait()
    near.wait()


def padded_column(c):
    a = max(a for a in range(HEAD_DIM) if CANON[a] <= c)
    return STARTS[a] + a % 8 + c - CANON[a]


def windows(features, nh):
    wide = features // nh
    ends = [(padded_column(k * wide), padded_column(k * wide + wide - 1)) for k in range(nh)]
    width = max(-(-(hi + 1) // 128) * 128 - lo // 128 * 128 for lo, hi in ends)
    return [min(lo // 128 * 128, PADDED - width) for lo, _ in ends], width


def window_at(starts, owner, nh):
    at = starts[0]
    for k in range(1, nh):
        at = at + (starts[k] - starts[k - 1]) * ((owner + nh - k) // nh)
    return at


def masked(full, causal):
    n = full.shape[0]
    last = jnp.where(causal, full[n - CHUNK :], 0.0)
    if n == CHUNK:
        return last.astype(BF16)
    return jnp.concatenate([full[: n - CHUNK], last], axis=0).astype(BF16)


def main_kernel(ns, nh, names, starts, width, *refs):
    r = dict(zip(names, refs))
    q_ref, kv_ref, init_ref, og_ref = r["q"], r["kv"], r["init"], r["og"]
    kvt, xs, x, row, df, f_all = r["kvt"], r["xs"], r["x"], r["row"], r["df"], r["f"]
    qt, ogt, attt, qgt, dnt = r["qt"], r["ogt"], r["attt"], r["qgt"], r["dnt"]
    start, startt, keys, vals, kt, vt = (
        r["start"], r["startt"], r["keys"], r["vals"], r["kt"], r["vt"]
    )
    carry, later_ref, sg, kvl = r["carry"], r["later"], r["sg"], r["kvl"]
    padt, tall = r["padt"], r["tall"]
    tokens = q_ref.shape[0]
    heads = q_ref.shape[1] // HEAD_DIM
    chunks = tokens // CHUNK
    features = init_ref.shape[1]
    rows, quarter, half, groups = HEAD_DIM // nh, tokens // nh, HEAD_DIM // nh // 2, ns // 2
    s, h, g, p, beside, partner, ring, across = places(ns, nh)
    links = Links(r["sends"], r["recvs"])
    barrier = pltpu.get_barrier_semaphore()
    for device in [partner] + ring + across:
        pl.semaphore_signal(barrier, inc=1, device_id=device, device_id_type=MESH)

    kvt[...] = kv_ref[...].astype(F32).T
    mine_vals = kvt[block(HEAD_DIM // rows + h, rows), :].astype(BF16)
    u_ref = r["u"]
    for c in range(chunks):
        at = slice(c * CHUNK, (c + 1) * CHUNK)
        xk = kvt.at[:HEAD_DIM, at]
        xs[...] = scaled(xk[...])
        write_features(xk, xs, f_all.at[c], CHUNK)
        part = dot(mine_vals[:, at], f_all[c], ((1,), (1,)))
        if c == 0:
            u_ref[...] = part
        else:
            u_ref[...] += part
    pl.semaphore_wait(barrier, 1 + len(ring) + len(across))
    pair = r["pair"]
    swap = links.copy(u_ref.at[block(1 - p, half), :], pair, partner)
    swap.start()

    qt[...] = q_ref[...].astype(F32).T
    kt[...] = kvt[:HEAD_DIM, :].astype(BF16)
    vt[...] = kvt[HEAD_DIM:, :].astype(BF16)
    keys[...] = kv_ref[:, :HEAD_DIM]
    vals[...] = kv_ref[:, HEAD_DIM:]
    causal = lax.broadcasted_iota(jnp.int32, (CHUNK, CHUNK), 0) <= lax.broadcasted_iota(
        jnp.int32, (CHUNK, CHUNK), 1
    )

    def inner(c):
        n = (c + 1) * CHUNK
        at = slice(c * CHUNK, n)

        def one_head(k, _):
            here = pl.ds(pl.multiple_of(k * HEAD_DIM, HEAD_DIM), HEAD_DIM)
            query = qt[here, at]
            x[...] = query
            xs[...] = scaled(query)
            write_features(x, xs, f_all.at[c * heads + k], CHUNK)
            logits = dot(keys[:n], query.astype(BF16))
            weights = masked(logits * logits * (1.0 / HEAD_DIM), causal)
            r[f"logits{c}"][k] = logits
            r[f"weights{c}"][k] = weights
            attt[here, at] = dot(vt[:, :n], weights)
            return 0

        lax.fori_loop(0, heads, one_head, 0)

    def upward(c):
        n = (c + 1) * CHUNK
        at = slice(c * CHUNK, n)

        def one_head(k, _):
            here = pl.ds(pl.multiple_of(k * HEAD_DIM, HEAD_DIM), HEAD_DIM)
            query = qt[here, at]
            xs[...] = scaled(query)
            dn = dnt[here, at]
            df[...] = dot(startt[...], dn)
            dw = dot(vals[:n], dn)
            dl = masked(dw * r[f"logits{c}"][k] * (2.0 / HEAD_DIM), causal)
            qgt[here, at] = dot(kt[:, :n], dl) + feature_grad(xs, df, row, CHUNK)
            kvl[:n, :HEAD_DIM] += dot(dl, query.astype(BF16), ((1,), (1,)))
            kvl[:n, HEAD_DIM:] += dot(r[f"weights{c}"][k], dn, ((1,), (1,)))
            return 0

        lax.fori_loop(0, heads, one_head, 0)

    swap.wait()
    both = r["both"]
    mine = u_ref[block(p, half), :]
    both[...] = mine + pair[...]
    moves = [links.copy(both, r["got"].at[k], ring[k]) for k in range(groups - 1)]
    for k, move in enumerate(moves):
        @pl.when(g + k + 1 < groups)
        def _(move=move):
            move.start()
    order = list(range(chunks))
    inner(order[-1])
    for c in order[:-3]:
        inner(c)
    ours = block(h * 2 + p, half)
    mate = r["mate"]
    base, mated = jnp.where(p == 1, pair[...], 0.0), jnp.where(p == 0, mine, 0.0)
    carry[ours, :] = base
    mate[...] = mated
    for k, move in enumerate(moves):
        @pl.when(g - k - 1 >= 0)
        def _(move=move, k=k):
            move.wait_recv()
            carry[ours, :] += r["got"][k]
            mate[...] += r["got"][k]
    back = links.copy(mate, carry.at[ours, :], partner)
    back.start()
    own_half = spread_piece(links, nh, s, h, beside, carry, half, p)
    start_gather(own_half)
    inner(order[-3])
    other_half = spread_piece(links, nh, s, h, beside, carry, half, 1 - p)
    back.wait_recv()
    start_gather(other_half)
    forward_gather(own_half)
    inner(order[-2])
    forward_gather(other_half)

    wide = r["wide"]
    whole_lanes = features // 128 * 128
    padt[...] = jnp.zeros_like(padt)
    wide[:, whole_lanes:] = jnp.zeros_like(wide[:, whole_lanes:])
    wide[:, :features] = init_ref[...]
    tall[...] = wide[...].T
    for a in range(HEAD_DIM):
        at = STARTS[a] + a % 8
        padt[at : at + HEAD_DIM - a, :] = tall[CANON[a] : CANON[a] + HEAD_DIM - a, :]
    initp = padt[...].T
    ogt[...] = og_ref[...].astype(F32).T
    for k, move in enumerate(moves):
        @pl.when(g + k + 1 < groups)
        def _(move=move):
            move.wait_send()
    back.wait_send()
    finish_gather(own_half)
    finish_gather(other_half)
    first_state = initp + carry[...]
    start[...] = first_state.astype(BF16)
    startt[...] = first_state.T.astype(BF16)

    sg[...] = jnp.zeros_like(sg)

    def normalize(i, _):
        c, k = i // heads, lax.rem(i, heads)
        here = pl.ds(pl.multiple_of(k * HEAD_DIM, HEAD_DIM), HEAD_DIM)
        at = pl.ds(pl.multiple_of(c * CHUNK, CHUNK), CHUNK)
        numer = attt[here, at] + dot(start[...], f_all[i])
        scale = lax.rsqrt(jnp.mean(numer * numer, axis=0, keepdims=True) + EPS)
        normed = numer * scale
        up = ogt[here, at]
        attt[here, at] = normed
        dn = (scale * (up - normed * jnp.mean(up * normed, axis=0, keepdims=True))).astype(BF16)
        dnt[here, at] = dn
        sg[...] += dot(dn, f_all[i], ((1,), (1,)))
        return 0

    lax.fori_loop(0, chunks * heads, normalize, 0)

    near, far, mid, own = r["near"], r["far"], r["mid"], r["own"]
    evens = range(2, nh + 1, 2)
    first, second = [], []
    for i, k in enumerate(evens):
        src = sg.at[block(lax.rem(beside + k, nh), rows), :]
        first.append(links.copy(src, near.at[i], (s, beside)))
        first[-1].start()
    kvl[...] = jnp.zeros_like(kvl)
    upward(0)
    for i, k in enumerate(evens):
        first[i].wait_recv()
        summed = sg[block(lax.rem(h + k, nh), rows), :] + near[i]
        if k == nh:
            own[...] = summed
        else:
            mid[i] = summed
            second.append(links.copy(mid.at[i], far.at[i], (s, lax.rem(h + k, nh))))
            second[-1].start()
    for c in order[1:-2]:
        upward(c)
    for i, copy in enumerate(second):
        copy.wait_recv()
        own[...] += far[i]
    spair, sboth = r["spair"], r["sboth"]
    sswap = links.copy(own.at[block(1 - p, half), :], spair, partner)
    sswap.start()
    att_ref, qg_ref = r["att"], r["qg"]
    upward(order[-2])
    sswap.wait()
    mine = own[block(p, half), :]
    sboth[...] = mine + spair[...]
    smoves = [links.copy(sboth, r["sgot"].at[k], ring[k]) for k in range(groups - 1)]
    for move in smoves:
        move.start()
    upward(order[-1])
    kvparts, kvscatter = r["kvparts"], []
    for k in range(nh - 1):
        src = kvl.at[block(lax.rem(h + k + 1, nh), quarter), :]
        kvscatter.append(links.copy(src, kvparts.at[k], across[k]))
        kvscatter[-1].start()
    smate, tot, total_ref = r["smate"], r["tot"], r["total"]
    later = jnp.where(p == 0, spair[...], 0.0)
    mated = jnp.where(p == 1, mine, 0.0)
    whole = sboth[...]
    for k, move in enumerate(smoves):
        move.wait_recv()
        whole = whole + r["sgot"][k]
        after = jnp.where(k + 1 > g, r["sgot"][k], 0.0)
        later = later + after
        mated = mated + after
    later_ref[ours, :] = later
    smate[...] = mated
    tot[...] = whole
    sback = links.copy(smate, later_ref.at[ours, :], partner)
    sback.start()
    own_half = spread_piece(links, nh, s, h, beside, later_ref, half, p)
    start_gather(own_half)
    total_swap = links.copy(tot, total_ref.at[block(p, half), :], partner)
    total_swap.start()
    other_half = spread_piece(links, nh, s, h, beside, later_ref, half, 1 - p)
    kq, vq = r["kq"], r["vq"]
    kvq = kv_ref[pl.ds(pl.multiple_of(h * quarter, 16), quarter), :].astype(F32).T
    kq[...] = kvq[:HEAD_DIM]
    vq[...] = kvq[HEAD_DIM:].astype(BF16)
    xs[...] = scaled(kq[...])
    write_features(kq, xs, f_all.at[0], quarter)
    sback.wait_recv()
    start_gather(other_half)
    total_ref[block(p, half), :] = tot[...]
    forward_gather(own_half)
    att_ref[...] = attt[...].T.astype(BF16)
    forward_gather(other_half)
    qg_ref[...] = qgt[...].T.astype(BF16)
    kvsum = kvl[block(h, quarter), :]
    for k, copy in enumerate(kvscatter):
        copy.wait()
        kvsum = kvsum + kvparts[k]
    r["kvsum"][...] = kvsum
    for copy in first + second + smoves + [sback]:
        copy.wait_send()
    total_swap.wait()
    finish_gather(own_half)
    finish_gather(other_half)

    win = r["win"]
    wins = []
    for k in range(nh - 1):
        to = lax.rem(h + k + 1, nh)
        columns = pl.ds(pl.multiple_of(window_at(starts, to, nh), 128), width)
        wins.append(links.copy(total_ref.at[:, columns], win.at[block(h, rows), :], across[k]))
        wins[-1].start()
    own_window = pl.ds(pl.multiple_of(window_at(starts, h, nh), 128), width)
    win[block(h, rows), :] = total_ref[:, own_window]
    later_state = later_ref[...]
    start[...] = later_state.astype(BF16)
    startt[...] = later_state.T.astype(BF16)
    gt = r["gt"]
    gt[HEAD_DIM:, :] = dot(start[...], f_all[0])
    df[...] = dot(startt[...], vq[...])
    gt[:HEAD_DIM, :] = feature_grad(xs, df, row, quarter)
    part_ref, kv_out = r["part"], r["kv_grad"]
    part_ref[...] = r["kvsum"][...] + gt[...].T
    spot = lambda owner: block(owner, quarter)
    parts = gather_copies(links, nh, s, h, beside, part_ref, kv_out, quarter, spot)
    start_gather(parts)
    kv_out[spot(h), :] = part_ref[...]
    for move in wins:
        move.wait()
    padt[own_window, :] = win[...].T
    forward_gather(parts)
    canon = r["tall"]
    for a in range(HEAD_DIM):
        at = STARTS[a] + a % 8
        canon[CANON[a] : CANON[a] + HEAD_DIM - a, :] = padt[at : at + HEAD_DIM - a, :]
    slice_width = features // nh
    flip, init_out = r["flip"], r["init_grad"]
    flip[:slice_width, :] = canon[block(h, slice_width), :]
    init_out[...] = flip[...].T[:, :slice_width]
    finish_gather(parts)


def per_device(ns, nh, queries, keys_values, init_state, out_grad):
    tokens, wide = queries.shape
    assert tokens == GROUP and ns % 2 == 0 and nh % 2 == 0 and tokens // nh == CHUNK
    features = init_state.shape[1]
    heads = wide // HEAD_DIM
    rows, quarter, groups = HEAD_DIM // nh, tokens // nh, ns // 2
    even = -(-features // 128) * 128
    starts, width = windows(features, nh)
    slice_width = features // nh
    D, V = pltpu.SemaphoreType.DMA, pltpu.VMEM
    part, piece, state = (rows, PADDED), (rows // 2, PADDED), (HEAD_DIM, PADDED)
    columns, chunk = (wide, tokens), (HEAD_DIM, CHUNK)
    count = 2 + groups - 1 + 2 * (nh - 1)
    count += nh // 2 + nh // 2 - 1 + nh - 1 + 3 + groups - 1 + 2 * (nh - 1)
    count += nh - 1 + nh - 1
    outs = dict(
        att=((tokens, wide), BF16),
        qg=((tokens, wide), BF16),
        kv_grad=((tokens, 2 * HEAD_DIM), F32),
        init_grad=((HEAD_DIM, slice_width), F32),
    )
    scratch = dict(
        kvt=V((2 * HEAD_DIM, tokens), F32), x=V(chunk, F32), xs=V(chunk, F32), row=V(chunk, F32),
        df=V((PADDED, CHUNK), F32), f=V((tokens // CHUNK * heads, PADDED, CHUNK), BF16),
        qt=V(columns, F32), ogt=V(columns, F32), attt=V(columns, F32), qgt=V(columns, F32),
        dnt=V(columns, BF16), start=V(state, BF16), startt=V((PADDED, HEAD_DIM), BF16),
        keys=V((tokens, HEAD_DIM), BF16), vals=V((tokens, HEAD_DIM), BF16),
        kt=V((HEAD_DIM, tokens), BF16), vt=V((HEAD_DIM, tokens), BF16),
        carry=V(state, F32), later=V(state, F32), sg=V(state, F32),
        kvl=V((tokens, 2 * HEAD_DIM), F32), padt=V((PADDED, HEAD_DIM), F32),
        tall=V((even, HEAD_DIM), F32), wide=V((HEAD_DIM, even), F32),
        u=V(part, F32), pair=V(piece, F32), both=V(piece, F32), mate=V(piece, F32),
        got=V((groups - 1,) + piece, F32),
        near=V((nh // 2,) + part, F32), far=V((nh // 2,) + part, F32),
        mid=V((nh // 2,) + part, F32), own=V(part, F32), spair=V(piece, F32),
        sboth=V(piece, F32), smate=V(piece, F32), tot=V(piece, F32), total=V(part, F32),
        sgot=V((groups - 1,) + piece, F32), kvparts=V((nh - 1, quarter, 2 * HEAD_DIM), F32),
        kq=V((HEAD_DIM, quarter), F32), vq=V((HEAD_DIM, quarter), BF16),
        kvsum=V((quarter, 2 * HEAD_DIM), F32), gt=V((2 * HEAD_DIM, quarter), F32),
        part=V((quarter, 2 * HEAD_DIM), F32), win=V((HEAD_DIM, width), F32),
        flip=V((-(-slice_width // 128) * 128, HEAD_DIM), F32),
        sends=D((count,)), recvs=D((count,)),
    )
    for c in range(tokens // CHUNK):
        scratch[f"logits{c}"] = V((heads, (c + 1) * CHUNK, CHUNK), F32)
        scratch[f"weights{c}"] = V((heads, (c + 1) * CHUNK, CHUNK), BF16)
    names = ["q", "kv", "init", "og"] + list(outs) + list(scratch)
    vmem = pl.BlockSpec(memory_space=pltpu.VMEM)
    return pl.pallas_call(
        functools.partial(main_kernel, ns, nh, names, starts, width),
        out_shape=tuple(jax.ShapeDtypeStruct(*out) for out in outs.values()),
        in_specs=[vmem] * 4,
        out_specs=(vmem,) * len(outs),
        scratch_shapes=list(scratch.values()),
        compiler_params=pltpu.CompilerParams(
            vmem_limit_bytes=62 * 1024 * 1024, collective_id=1, has_side_effects=True
        ),
    )(queries, keys_values, init_state, out_grad)


def solution(mesh):
    ns, nh = mesh.shape["seq"], mesh.shape["head"]
    return jax.shard_map(
        functools.partial(per_device, ns, nh),
        mesh=mesh,
        in_specs=(P("seq", "head"), P("seq", None), P(), P("seq", "head")),
        out_specs=(P("seq", "head"), P("seq", "head"), P("seq", None), P(None, "head")),
        check_vma=False,
    )
```

```python
import functools

import jax
import jax.numpy as jnp
import numpy as np
from jax import lax
from jax.experimental import pallas as pl
from jax.experimental.pallas import tpu as pltpu
from jax.sharding import PartitionSpec as P

HEAD_DIM = 64
GROUP = 1024
EPS = 1e-06
CHUNK = 256
MESH = pl.DeviceIdType.MESH
F32, BF16 = jnp.float32, jnp.bfloat16


def padded_layout(width):
    starts, at = [], 0
    for a in range(width):
        starts.append(at)
        at += width - a // 8 * 8
    return starts, at


STARTS, PADDED = padded_layout(HEAD_DIM)
CANON = [a * HEAD_DIM - a * (a - 1) // 2 for a in range(HEAD_DIM)]


def dot(first, second, contract=((1,), (0,))):
    return lax.dot_general(first, second, (contract, ((), ())), preferred_element_type=F32)


def edge_weights(cols):
    row = lax.broadcasted_iota(jnp.int32, (8, cols), 0)
    return [
        jnp.where(row < m, 0.0, jnp.where(row == m, float(np.sqrt(0.5)), 1.0)).astype(F32)
        for m in range(8)
    ]


def write_features(x_ref, xs_ref, f_ref, cols):
    edges = edge_weights(cols)
    for a in range(0, HEAD_DIM, 2):
        base = a // 8 * 8
        parts = []
        for c in (a, a + 1):
            prod = x_ref[c : c + 1, :] * xs_ref[base:, :]
            parts.append(prod[:8] * edges[c % 8])
            if base + 8 < HEAD_DIM:
                parts.append(prod[8:])
        at = STARTS[a]
        f_ref[at : at + 2 * (HEAD_DIM - base), :] = jnp.concatenate(parts, axis=0).astype(BF16)


def feature_grad(xs_ref, df_ref, row_ref, cols):
    edges = edge_weights(cols)
    tiles = HEAD_DIM // 8
    acc = [jnp.zeros((8, cols), F32) for _ in range(tiles)]
    for a in range(HEAD_DIM):
        first = a // 8
        xa = jnp.broadcast_to(xs_ref[a : a + 1, :], (8, cols))
        total = None
        for t in range(first, tiles):
            at = STARTS[a] + (t - first) * 8
            part = df_ref[at : at + 8, :]
            if t == first:
                part = part * edges[a % 8]
            acc[t] = acc[t] + part * xa
            term = part * xs_ref[t * 8 : t * 8 + 8, :]
            total = term if total is None else total + term
        row_ref[a : a + 1, :] = jnp.sum(total, axis=0, keepdims=True)
    return jnp.concatenate(acc, axis=0) + row_ref[...]


def scaled(x):
    return x * float(np.sqrt(2.0 / HEAD_DIM))


def places(ns, nh):
    s, h = lax.axis_index("seq"), lax.axis_index("head")
    groups = ns // 2
    g, p = s // 2, s % 2
    beside = h + 1 - 2 * (h % 2)
    partner = (s + 1 - 2 * p, h)
    ring = [(lax.rem(g + k, groups) * 2 + p, h) for k in range(1, groups)]
    across = [(s, lax.rem(h + k, nh)) for k in range(1, nh)]
    return s, h, g, p, beside, partner, ring, across


def block(index, size):
    return pl.ds(pl.multiple_of(index * size, 8), size)


class Links:
    def __init__(self, sends, recvs):
        self.sends, self.recvs, self.used = sends, recvs, 0

    def copy(self, src, dst, device):
        k = self.used
        self.used += 1
        return pltpu.make_async_remote_copy(
            src_ref=src, dst_ref=dst, send_sem=self.sends.at[k], recv_sem=self.recvs.at[k],
            device_id=device, device_id_type=MESH,
        )


def gather_copies(links, nh, s, h, beside, src, out, size, spot):
    far = []
    for k in range(2, nh, 2):
        to = lax.rem(h + k, nh)
        first = links.copy(src, out.at[spot(h)], (s, to))
        came = out.at[spot(lax.rem(h + nh - k, nh))]
        far.append((first, links.copy(came, came, (s, beside))))
    near = links.copy(src, out.at[spot(h)], (s, beside))
    return far, near


def spread_piece(links, nh, s, h, beside, out, half, slot):
    spot = lambda owner: block(owner * 2 + slot, half)
    return gather_copies(links, nh, s, h, beside, out.at[spot(h)], out, half, spot)


def start_gather(gather):
    far, near = gather
    for first, _ in far:
        first.start()
    near.start()


def forward_gather(gather):
    for first, second in gather[0]:
        first.wait_recv()
        second.start()


def finish_gather(gather):
    far, near = gather
    for first, second in far:
        first.wait_send()
        second.wait()
    near.wait()


def padded_column(c):
    a = max(a for a in range(HEAD_DIM) if CANON[a] <= c)
    return STARTS[a] + a % 8 + c - CANON[a]


def windows(features, nh):
    wide = features // nh
    ends = [(padded_column(k * wide), padded_column(k * wide + wide - 1)) for k in range(nh)]
    width = max(-(-(hi + 1) // 128) * 128 - lo // 128 * 128 for lo, hi in ends)
    return [min(lo // 128 * 128, PADDED - width) for lo, _ in ends], width


def window_at(starts, owner, nh):
    at = starts[0]
    for k in range(1, nh):
        at = at + (starts[k] - starts[k - 1]) * ((owner + nh - k) // nh)
    return at


def masked(full, causal):
    n = full.shape[0]
    last = jnp.where(causal, full[n - CHUNK :], 0.0)
    if n == CHUNK:
        return last.astype(BF16)
    return jnp.concatenate([full[: n - CHUNK], last], axis=0).astype(BF16)


def main_kernel(ns, nh, names, starts, width, *refs):
    r = dict(zip(names, refs))
    q_ref, kv_ref, init_ref, og_ref = r["q"], r["kv"], r["init"], r["og"]
    kvt, xs, x, row, df, f_all = r["kvt"], r["xs"], r["x"], r["row"], r["df"], r["f"]
    qt, ogt, attt, qgt, dnt = r["qt"], r["ogt"], r["attt"], r["qgt"], r["dnt"]
    start, startt, keys, vals, kt, vt = (
        r["start"], r["startt"], r["keys"], r["vals"], r["kt"], r["vt"]
    )
    carry, later_ref, sg, kvl = r["carry"], r["later"], r["sg"], r["kvl"]
    padt, tall = r["padt"], r["tall"]
    tokens = q_ref.shape[0]
    heads = q_ref.shape[1] // HEAD_DIM
    chunks = tokens // CHUNK
    features = init_ref.shape[1]
    rows, quarter, half, groups = HEAD_DIM // nh, tokens // nh, HEAD_DIM // nh // 2, ns // 2
    s, h, g, p, beside, partner, ring, across = places(ns, nh)
    links = Links(r["sends"], r["recvs"])
    barrier = pltpu.get_barrier_semaphore()
    for device in [partner] + ring + across:
        pl.semaphore_signal(barrier, inc=1, device_id=device, device_id_type=MESH)

    kvt[...] = kv_ref[...].astype(F32).T
    mine_vals = kvt[block(HEAD_DIM // rows + h, rows), :].astype(BF16)
    u_ref = r["u"]
    for c in range(chunks):
        at = slice(c * CHUNK, (c + 1) * CHUNK)
        xk = kvt.at[:HEAD_DIM, at]
        xs[...] = scaled(xk[...])
        write_features(xk, xs, f_all.at[c], CHUNK)
        part = dot(mine_vals[:, at], f_all[c], ((1,), (1,)))
        if c == 0:
            u_ref[...] = part
        else:
            u_ref[...] += part
    pl.semaphore_wait(barrier, 1 + len(ring) + len(across))
    pair = r["pair"]
    swap = links.copy(u_ref.at[block(1 - p, half), :], pair, partner)
    swap.start()

    qt[...] = q_ref[...].astype(F32).T
    kt[...] = kvt[:HEAD_DIM, :].astype(BF16)
    vt[...] = kvt[HEAD_DIM:, :].astype(BF16)
    keys[...] = kv_ref[:, :HEAD_DIM]
    vals[...] = kv_ref[:, HEAD_DIM:]
    causal = lax.broadcasted_iota(jnp.int32, (CHUNK, CHUNK), 0) <= lax.broadcasted_iota(
        jnp.int32, (CHUNK, CHUNK), 1
    )

    def inner(c):
        n = (c + 1) * CHUNK
        at = slice(c * CHUNK, n)

        def one_head(k, _):
            here = pl.ds(pl.multiple_of(k * HEAD_DIM, HEAD_DIM), HEAD_DIM)
            query = qt[here, at]
            x[...] = query
            xs[...] = scaled(query)
            write_features(x, xs, f_all.at[c * heads + k], CHUNK)
            logits = dot(keys[:n], query.astype(BF16))
            weights = masked(logits * logits * (1.0 / HEAD_DIM), causal)
            r[f"logits{c}"][k] = logits
            r[f"weights{c}"][k] = weights
            attt[here, at] = dot(vt[:, :n], weights)
            return 0

        lax.fori_loop(0, heads, one_head, 0)

    def upward(c):
        n = (c + 1) * CHUNK
        at = slice(c * CHUNK, n)

        def one_head(k, _):
            here = pl.ds(pl.multiple_of(k * HEAD_DIM, HEAD_DIM), HEAD_DIM)
            query = qt[here, at]
            xs[...] = scaled(query)
            dn = dnt[here, at]
            df[...] = dot(startt[...], dn)
            dw = dot(vals[:n], dn)
            dl = masked(dw * r[f"logits{c}"][k] * (2.0 / HEAD_DIM), causal)
            qgt[here, at] = dot(kt[:, :n], dl) + feature_grad(xs, df, row, CHUNK)
            kvl[:n, :HEAD_DIM] += dot(dl, query.astype(BF16), ((1,), (1,)))
            kvl[:n, HEAD_DIM:] += dot(r[f"weights{c}"][k], dn, ((1,), (1,)))
            return 0

        lax.fori_loop(0, heads, one_head, 0)

    wide = r["wide"]
    whole_lanes = features // 128 * 128
    padt[...] = jnp.zeros_like(padt)
    wide[:, whole_lanes:] = jnp.zeros_like(wide[:, whole_lanes:])
    wide[:, :features] = init_ref[...]
    tall[...] = wide[...].T
    for a in range(HEAD_DIM):
        at = STARTS[a] + a % 8
        padt[at : at + HEAD_DIM - a, :] = tall[CANON[a] : CANON[a] + HEAD_DIM - a, :]
    r["initp"][...] = padt[...].T
    ogt[...] = og_ref[...].astype(F32).T
    swap.wait()
    both = r["both"]
    mine = u_ref[block(p, half), :]
    both[...] = mine + pair[...]
    moves = [links.copy(both, r["got"].at[k], ring[k]) for k in range(groups - 1)]
    for k, move in enumerate(moves):
        @pl.when(g + k + 1 < groups)
        def _(move=move):
            move.start()
    order = list(range(chunks))
    inner(order[-1])
    for c in order[:-3]:
        inner(c)
    ours = block(h * 2 + p, half)
    mate = r["mate"]
    base, mated = jnp.where(p == 1, pair[...], 0.0), jnp.where(p == 0, mine, 0.0)
    carry[ours, :] = base
    mate[...] = mated
    for k, move in enumerate(moves):
        @pl.when(g - k - 1 >= 0)
        def _(move=move, k=k):
            move.wait_recv()
            carry[ours, :] += r["got"][k]
            mate[...] += r["got"][k]
    back = links.copy(mate, carry.at[ours, :], partner)
    back.start()
    own_half = spread_piece(links, nh, s, h, beside, carry, half, p)
    start_gather(own_half)
    inner(order[-3])
    other_half = spread_piece(links, nh, s, h, beside, carry, half, 1 - p)
    back.wait_recv()
    start_gather(other_half)
    forward_gather(own_half)
    inner(order[-2])
    forward_gather(other_half)

    for k, move in enumerate(moves):
        @pl.when(g + k + 1 < groups)
        def _(move=move):
            move.wait_send()
    back.wait_send()
    finish_gather(own_half)
    finish_gather(other_half)
    first_state = r["initp"][...] + carry[...]
    start[...] = first_state.astype(BF16)
    startt[...] = first_state.T.astype(BF16)

    sg[...] = jnp.zeros_like(sg)

    def normalize(i, _):
        c, k = i // heads, lax.rem(i, heads)
        here = pl.ds(pl.multiple_of(k * HEAD_DIM, HEAD_DIM), HEAD_DIM)
        at = pl.ds(pl.multiple_of(c * CHUNK, CHUNK), CHUNK)
        numer = attt[here, at] + dot(start[...], f_all[i])
        scale = lax.rsqrt(jnp.mean(numer * numer, axis=0, keepdims=True) + EPS)
        normed = numer * scale
        up = ogt[here, at]
        attt[here, at] = normed
        dn = (scale * (up - normed * jnp.mean(up * normed, axis=0, keepdims=True))).astype(BF16)
        dnt[here, at] = dn
        sg[...] += dot(dn, f_all[i], ((1,), (1,)))
        return 0

    lax.fori_loop(0, chunks * heads, normalize, 0)

    near, far, mid, own = r["near"], r["far"], r["mid"], r["own"]
    evens = range(2, nh + 1, 2)
    first, second = [], []
    for i, k in enumerate(evens):
        src = sg.at[block(lax.rem(beside + k, nh), rows), :]
        first.append(links.copy(src, near.at[i], (s, beside)))
        first[-1].start()
    kvl[...] = jnp.zeros_like(kvl)
    upward(0)
    for i, k in enumerate(evens):
        first[i].wait_recv()
        summed = sg[block(lax.rem(h + k, nh), rows), :] + near[i]
        if k == nh:
            own[...] = summed
        else:
            mid[i] = summed
            second.append(links.copy(mid.at[i], far.at[i], (s, lax.rem(h + k, nh))))
            second[-1].start()
    for c in order[1:-2]:
        upward(c)
    for i, copy in enumerate(second):
        copy.wait_recv()
        own[...] += far[i]
    spair, sboth = r["spair"], r["sboth"]
    sswap = links.copy(own.at[block(1 - p, half), :], spair, partner)
    sswap.start()
    att_ref, qg_ref = r["att"], r["qg"]
    upward(order[-2])
    sswap.wait()
    mine = own[block(p, half), :]
    sboth[...] = mine + spair[...]
    smoves = [links.copy(sboth, r["sgot"].at[k], ring[k]) for k in range(groups - 1)]
    for move in smoves:
        move.start()
    upward(order[-1])
    kvnear, kvfar, kvmid = r["kvnear"], r["kvfar"], r["kvmid"]
    kvfirst, kvsecond = [], []
    for i, k in enumerate(evens):
        src = kvl.at[block(lax.rem(beside + k, nh), quarter), :]
        kvfirst.append(links.copy(src, kvnear.at[i], (s, beside)))
        kvfirst[-1].start()
    smate, tot, total_ref = r["smate"], r["tot"], r["total"]
    later = jnp.where(p == 0, spair[...], 0.0)
    mated = jnp.where(p == 1, mine, 0.0)
    whole = sboth[...]
    for k, move in enumerate(smoves):
        move.wait_recv()
        whole = whole + r["sgot"][k]
        after = jnp.where(k + 1 > g, r["sgot"][k], 0.0)
        later = later + after
        mated = mated + after
    later_ref[ours, :] = later
    smate[...] = mated
    tot[...] = whole
    sback = links.copy(smate, later_ref.at[ours, :], partner)
    sback.start()
    own_half = spread_piece(links, nh, s, h, beside, later_ref, half, p)
    start_gather(own_half)
    total_swap = links.copy(tot, total_ref.at[block(p, half), :], partner)
    total_swap.start()
    other_half = spread_piece(links, nh, s, h, beside, later_ref, half, 1 - p)
    kq, vq = r["kq"], r["vq"]
    kvq = kv_ref[pl.ds(pl.multiple_of(h * quarter, 16), quarter), :].astype(F32).T
    kq[...] = kvq[:HEAD_DIM]
    vq[...] = kvq[HEAD_DIM:].astype(BF16)
    xs[...] = scaled(kq[...])
    write_features(kq, xs, f_all.at[0], quarter)
    sback.wait_recv()
    start_gather(other_half)
    for i, k in enumerate(evens):
        kvfirst[i].wait_recv()
        summed = kvl[block(lax.rem(h + k, nh), quarter), :] + kvnear[i]
        if k == nh:
            r["kvsum"][...] = summed
        else:
            kvmid[i] = summed
            to = (s, lax.rem(h + k, nh))
            kvsecond.append(links.copy(kvmid.at[i], kvfar.at[i], to))
            kvsecond[-1].start()
    total_ref[block(p, half), :] = tot[...]
    forward_gather(own_half)
    att_ref[...] = attt[...].T.astype(BF16)
    forward_gather(other_half)
    qg_ref[...] = qgt[...].T.astype(BF16)
    for copy in first + second + smoves + kvfirst + [sback]:
        copy.wait_send()
    total_swap.wait()
    finish_gather(own_half)
    finish_gather(other_half)

    win = r["win"]
    wins = []
    for k in range(nh - 1):
        to = lax.rem(h + k + 1, nh)
        columns = pl.ds(pl.multiple_of(window_at(starts, to, nh), 128), width)
        wins.append(links.copy(total_ref.at[:, columns], win.at[block(h, rows), :], across[k]))
        wins[-1].start()
    own_window = pl.ds(pl.multiple_of(window_at(starts, h, nh), 128), width)
    win[block(h, rows), :] = total_ref[:, own_window]
    later_state = later_ref[...]
    start[...] = later_state.astype(BF16)
    startt[...] = later_state.T.astype(BF16)
    for i, copy in enumerate(kvsecond):
        copy.wait()
        r["kvsum"][...] += kvfar[i]
    gt, part_ref, kv_out = r["gt"], r["part"], r["kv_grad"]
    size = quarter // 2
    gathers = []
    for j in range(2):
        at = slice(j * size, (j + 1) * size)
        gt[HEAD_DIM:, at] = dot(start[...], f_all[0, :, at])
        df[:, at] = dot(startt[...], vq[:, at])
        gt[:HEAD_DIM, at] = feature_grad(xs.at[:, at], df.at[:, at], row.at[:, at], size)
        part_ref[at, :] = r["kvsum"][at, :] + gt[:, at].T
        spot = lambda owner, j=j: block(owner * 2 + j, size)
        gathers.append(gather_copies(links, nh, s, h, beside, part_ref.at[at, :], kv_out, size, spot))
        start_gather(gathers[-1])
    for move in wins:
        move.wait()
    padt[own_window, :] = win[...].T
    kv_out[block(h, quarter), :] = part_ref[...]
    forward_gather(gathers[0])
    canon = r["tall"]
    for a in range(HEAD_DIM):
        at = STARTS[a] + a % 8
        canon[CANON[a] : CANON[a] + HEAD_DIM - a, :] = padt[at : at + HEAD_DIM - a, :]
    slice_width = features // nh
    flip, init_out = r["flip"], r["init_grad"]
    flip[:slice_width, :] = canon[block(h, slice_width), :]
    forward_gather(gathers[1])
    init_out[...] = flip[...].T[:, :slice_width]
    for gather in gathers:
        finish_gather(gather)


def deliver_kernel(count, *refs):
    sems = refs[-1]
    copies = [pltpu.make_async_copy(refs[i], refs[count + i], sems.at[i]) for i in range(count)]
    for copy in copies:
        copy.start()
    for copy in copies:
        copy.wait()


def deliver(arrays):
    hbm = pl.BlockSpec(memory_space=pl.ANY)
    return pl.pallas_call(
        functools.partial(deliver_kernel, len(arrays)),
        out_shape=tuple(jax.ShapeDtypeStruct(x.shape, x.dtype) for x in arrays),
        in_specs=[hbm] * len(arrays),
        out_specs=(hbm,) * len(arrays),
        scratch_shapes=[pltpu.SemaphoreType.DMA((len(arrays),))],
    )(*arrays)


def per_device(ns, nh, queries, keys_values, init_state, out_grad):
    tokens, wide = queries.shape
    assert tokens == GROUP and ns % 2 == 0 and nh % 2 == 0 and tokens // nh == CHUNK
    features = init_state.shape[1]
    heads = wide // HEAD_DIM
    rows, quarter, groups = HEAD_DIM // nh, tokens // nh, ns // 2
    even = -(-features // 128) * 128
    starts, width = windows(features, nh)
    slice_width = features // nh
    D, V = pltpu.SemaphoreType.DMA, pltpu.VMEM
    part, piece, state = (rows, PADDED), (rows // 2, PADDED), (HEAD_DIM, PADDED)
    columns, chunk = (wide, tokens), (HEAD_DIM, CHUNK)
    count = 2 + groups - 1 + 2 * (nh - 1)
    count += 2 * (nh - 1) + 3 + groups - 1 + 2 * (nh - 1)
    count += 3 * (nh - 1)
    outs = dict(
        att=((tokens, wide), BF16),
        qg=((tokens, wide), BF16),
        kv_grad=((tokens, 2 * HEAD_DIM), F32),
        init_grad=((HEAD_DIM, slice_width), F32),
    )
    scratch = dict(
        kvt=V((2 * HEAD_DIM, tokens), F32), x=V(chunk, F32), xs=V(chunk, F32), row=V(chunk, F32),
        df=V((PADDED, CHUNK), F32), f=V((tokens // CHUNK * heads, PADDED, CHUNK), BF16),
        qt=V(columns, F32), ogt=V(columns, F32), attt=V(columns, F32), qgt=V(columns, F32),
        dnt=V(columns, BF16), start=V(state, BF16), startt=V((PADDED, HEAD_DIM), BF16),
        keys=V((tokens, HEAD_DIM), BF16), vals=V((tokens, HEAD_DIM), BF16),
        kt=V((HEAD_DIM, tokens), BF16), vt=V((HEAD_DIM, tokens), BF16),
        carry=V(state, F32), later=V(state, F32), sg=V(state, F32),
        kvl=V((tokens, 2 * HEAD_DIM), F32), padt=V((PADDED, HEAD_DIM), F32),
        tall=V((even, HEAD_DIM), F32), wide=V((HEAD_DIM, even), F32),
        u=V(part, F32), pair=V(piece, F32), both=V(piece, F32), mate=V(piece, F32),
        got=V((groups - 1,) + piece, F32),
        near=V((nh // 2,) + part, F32), far=V((nh // 2,) + part, F32),
        mid=V((nh // 2,) + part, F32), own=V(part, F32), spair=V(piece, F32),
        sboth=V(piece, F32), smate=V(piece, F32), tot=V(piece, F32), total=V(part, F32),
        sgot=V((groups - 1,) + piece, F32), kvnear=V((nh // 2, quarter, 2 * HEAD_DIM), F32),
        kvfar=V((nh // 2, quarter, 2 * HEAD_DIM), F32),
        kvmid=V((nh // 2, quarter, 2 * HEAD_DIM), F32),
        initp=V(state, F32),
        kq=V((HEAD_DIM, quarter), F32), vq=V((HEAD_DIM, quarter), BF16),
        kvsum=V((quarter, 2 * HEAD_DIM), F32), gt=V((2 * HEAD_DIM, quarter), F32),
        part=V((quarter, 2 * HEAD_DIM), F32), win=V((HEAD_DIM, width), F32),
        flip=V((-(-slice_width // 128) * 128, HEAD_DIM), F32),
        sends=D((count,)), recvs=D((count,)),
    )
    for c in range(tokens // CHUNK):
        scratch[f"logits{c}"] = V((heads, (c + 1) * CHUNK, CHUNK), F32)
        scratch[f"weights{c}"] = V((heads, (c + 1) * CHUNK, CHUNK), BF16)
    names = ["q", "kv", "init", "og"] + list(outs) + list(scratch)
    vmem = pl.BlockSpec(memory_space=pltpu.VMEM)
    results = pl.pallas_call(
        functools.partial(main_kernel, ns, nh, names, starts, width),
        out_shape=tuple(jax.ShapeDtypeStruct(*out) for out in outs.values()),
        in_specs=[vmem] * 4,
        out_specs=(vmem,) * len(outs),
        scratch_shapes=list(scratch.values()),
        compiler_params=pltpu.CompilerParams(
            vmem_limit_bytes=62 * 1024 * 1024, collective_id=1, has_side_effects=True
        ),
    )(queries, keys_values, init_state, out_grad)
    return deliver(results)


def solution(mesh):
    ns, nh = mesh.shape["seq"], mesh.shape["head"]
    return jax.shard_map(
        functools.partial(per_device, ns, nh),
        mesh=mesh,
        in_specs=(P("seq", "head"), P("seq", None), P(), P("seq", "head")),
        out_specs=(P("seq", "head"), P("seq", "head"), P("seq", None), P(None, "head")),
        check_vma=False,
    )
```
